32 devices in a mesh: ctx: 8 (over y, x, core), fsdp: 4 (over z).
Axes of the slice: x: 2, y: 2, z: 4, core: 2. Of those that a mesh axis runs over, the one named last changes fastest.
Arguments:
- layer_in: bfloat16 [8, 1024, 1024], P('fsdp', 'ctx'), may hold values from -6 to 6
- cotangent: bfloat16 [8, 1024, 1024], P('fsdp', 'ctx'), may hold values from -6 to 6
- norm1_gain: bfloat16 [1024], P('fsdp'), may hold values from 0.099609375 to 1.8984375
- norm1_shift: bfloat16 [1024], P('fsdp'), may hold values from -3 to 3
- norm2_gain: bfloat16 [1024], P('fsdp'), may hold values from 0.099609375 to 1.8984375
- norm2_shift: bfloat16 [1024], P('fsdp'), may hold values from -3 to 3
- qkv_weight: bfloat16 [1024, 3072], P('fsdp'), may hold values from -4 to 4
- qv_bias: bfloat16 [2048], P('fsdp'), may hold values from -3 to 3
- key_bias: bfloat16 [256], P('fsdp'), may hold values from -3 to 3
- attn_out_weight: bfloat16 [1024, 1024], P('fsdp'), may hold values from -1.5 to 1.5
- attn_out_bias: bfloat16 [1024], P('fsdp'), may hold values from -3 to 3
- ff_in_weight: bfloat16 [1024, 4096], P('fsdp'), may hold values from -0.1875 to 0.1875
- ff_in_bias: bfloat16 [4096], P('fsdp'), may hold values from -3 to 3
- ff_out_weight: bfloat16 [1024, 4096], P('fsdp'), may hold values from -0.09375 to 0.09375
- ff_out_bias: bfloat16 [1024], P('fsdp'), may hold values from -3 to 3
Outputs:
- layer_out: bfloat16 [8, 1024, 1024], P('fsdp', 'ctx')
- input_grad: float32 [8, 1024, 1024], P('fsdp', 'ctx')
- norm1_gain_grad: float32 [1024], P('fsdp')
- norm1_shift_grad: float32 [1024], P('fsdp')
- norm2_gain_grad: float32 [1024], P('fsdp')
- norm2_shift_grad: float32 [1024], P('fsdp')
- qkv_weight_grad: float32 [1024, 3072], P('fsdp')
- qv_bias_grad: float32 [2048], P('fsdp')
- key_bias_grad: float32 [256], P('fsdp')
- attn_out_weight_grad: float32 [1024, 1024], P('fsdp')
- attn_out_bias_grad: float32 [1024], P('fsdp')
- ff_in_weight_grad: float32 [1024, 4096], P('fsdp')
- ff_in_bias_grad: float32 [4096], P('fsdp')
- ff_out_weight_grad: float32 [1024, 4096], P('fsdp')
- ff_out_bias_grad: float32 [1024], P('fsdp')
The draws below stay inside these ranges and needn't reach their ends.
All inputs are finite; a program needn't handle non-finite values.
Results may differ from the reference program's by a relative error of at most 0.025.
Values may be sent and summed in bfloat16 or wider, within the bound.
A program may use at most 256 MiB of HBM per device.

```python
import math
import jax
import jax.numpy as jnp
from jax import lax

D = 1024
H = 16
HD = 64
ROT = 16
FF = 4096
LENGTH = 1024
BLK = 64
SEQS = 8
N_CTX = 8


def draw_qkv_weight(key, part):
    key_base = jax.random.fold_in(key, 0)
    spread_scale = 1.0 / D ** 0.5
    weights = jnp.clip(jax.random.normal(key_base, (D, 3 * D), jnp.float32), -6.0, 6.0) * spread_scale
    return weights.astype(jnp.bfloat16)


def spiked(values, own_key, source, target, shards_of, factor):
    def block_of(dim):
        return (jnp.arange(values.shape[dim]) // (values.shape[dim] // shards_of)).reshape((-1,) + (1,) * (values.ndim - 1 - dim))

    near = jax.random.permutation(own_key, shards_of)[block_of(target)]
    other_side = (block_of(target) + shards_of // 2) % shards_of
    return jnp.where((block_of(source) == near) | (block_of(source) == other_side), factor * values, values)


def steps_of(own_key, dims, cuts, smallest, high):
    level = 1.0
    for dim, blocks in cuts:
        draws = jax.random.uniform(jax.random.fold_in(jax.random.fold_in(own_key, 6), dim), (blocks,), jnp.float32, smallest / len(cuts), high / len(cuts))
        level = level * jnp.repeat(jnp.exp(draws), dims[dim] // blocks).reshape((-1,) + (1,) * (len(dims) - 1 - dim))
    return level


def normal_values(key, extent, spread, limit, cuts=(), held_as=jnp.bfloat16):
    gain = steps_of(key, extent, cuts, -0.22, 0.18) if cuts else 1.0
    array = jax.random.normal(key, extent, jnp.float32) * spread * gain
    return jnp.minimum(jnp.maximum(array, -limit), limit).astype(held_as)


def gaussian_with(own_key, extent, scale, bound, cuts, heavy, held_as=jnp.bfloat16):
    values = scale * jax.random.normal(own_key, extent, jnp.float32)
    if cuts:
        values = values * steps_of(own_key, extent, cuts, -0.22, 0.18)
    return jnp.clip(spiked(values, jax.random.fold_in(own_key, 3), *heavy), -bound, bound).astype(held_as)


def setup_inputs(seed: int = 0) -> dict:
    seeds = jax.random.split(jax.random.key(seed), 16)
    return {
        "layer_in": normal_values(seeds[0], (SEQS, LENGTH, D), 1.0, 6.0, ((0, 4), (1, 8))),
        "cotangent": gaussian_with(seeds[1], (SEQS, LENGTH, D), 1.0, 6.0, ((0, 4), (1, 8)), (1, 2, 8, 2.0)),
        "norm1_gain": jnp.clip(1.0 + 0.18 * jax.random.normal(seeds[2], (D,), jnp.float32), 0.099609375, 1.8984375).astype(jnp.bfloat16),
        "norm1_shift": normal_values(seeds[3], (D,), 0.3, 3.0, ((0, 4),)),
        "norm2_gain": jnp.clip(1.0 + 0.18 * jax.random.normal(seeds[4], (D,), jnp.float32), 0.099609375, 1.8984375).astype(jnp.bfloat16),
        "norm2_shift": normal_values(seeds[5], (D,), 0.3, 3.0, ((0, 4),)),
        "qkv_weight": draw_qkv_weight(jax.random.fold_in(seeds[15], 71), 0),
        "qv_bias": normal_values(seeds[7], (2 * D,), 0.5, 3.0, ((0, 4),)),
        "key_bias": normal_values(seeds[8], (H * ROT,), 0.5, 3.0, ((0, 4),)),
        "attn_out_weight": normal_values(seeds[9], (D, D), 16 ** -0.5, 1.5, ((0, 4),)),
        "attn_out_bias": normal_values(seeds[10], (D,), 0.3, 3.0, ((0, 4),)),
        "ff_in_weight": normal_values(seeds[11], (D, FF), D ** -0.5, 0.1875, ((0, 4),)),
        "ff_in_bias": normal_values(seeds[12], (FF,), 0.5, 3.0, ((0, 4),)),
        "ff_out_weight": normal_values(seeds[13], (D, FF), FF ** -0.5, 0.09375, ((0, 4),)),
        "ff_out_bias": normal_values(seeds[14], (D,), 0.3, 3.0, ((0, 4),)),
    }


EPSILON = 1e-05

def layer_norm(inputs, gain_vec, shift_vec):
    average = lax.optimization_barrier(jnp.mean(inputs, axis=-1, keepdims=True))
    centred = inputs - average
    variance = lax.optimization_barrier(jnp.mean(centred * centred, axis=-1, keepdims=True))
    inverse = lax.rsqrt(variance + EPSILON)
    normed = centred * inverse
    return (normed * gain_vec + shift_vec, normed, inverse)

def norm_back(upstream, normed, inverse, gain_vec):
    gain_grad = lax.optimization_barrier(jnp.sum(upstream * normed, axis=0))
    shift_grad = lax.optimization_barrier(jnp.sum(upstream, axis=0))
    scaled = upstream * gain_vec
    inner = scaled - lax.optimization_barrier(jnp.mean(scaled, axis=-1, keepdims=True)) - normed * lax.optimization_barrier(jnp.mean(scaled * normed, axis=-1, keepdims=True))
    return (inverse * inner, gain_grad, shift_grad)

def paired_position(row_ids, half_rows, groups):
    owner = row_ids // (2 * half_rows)
    within = row_ids % (2 * half_rows)
    late = 2 * half_rows * groups - (owner + 2) * half_rows + within
    return jnp.where(within < half_rows, owner * half_rows + within, late).astype(jnp.int32)

def rotary_tables(positions):
    halfway = ROT // 2
    freq_steps = jnp.arange(halfway, dtype=jnp.float32)
    frequency = jnp.exp(freq_steps * (-2.0 * math.log(10000.0) / ROT))
    theta = positions.astype(jnp.float32)[:, None] * frequency[None, :]
    return (jnp.cos(theta)[:, None, :], jnp.sin(theta)[:, None, :])

def rotate(inputs, cosine, sine):
    halfway = ROT // 2
    first = inputs[..., :halfway]
    second = inputs[..., halfway:ROT]
    return jnp.concatenate([first * cosine - second * sine, second * cosine + first * sine, inputs[..., ROT:]], axis=-1)

def rotate_back(upstream, cosine, sine):
    halfway = ROT // 2
    first = upstream[..., :halfway]
    second = upstream[..., halfway:ROT]
    return jnp.concatenate([first * cosine + second * sine, second * cosine - first * sine, upstream[..., ROT:]], axis=-1)

def gelu_parts(inputs):
    cumulative = 0.5 * (1.0 + lax.erf(inputs * (1.0 / math.sqrt(2.0))))
    density = jnp.exp(-0.5 * inputs * inputs) * (1.0 / math.sqrt(2.0 * math.pi))
    return (inputs * cumulative, cumulative + inputs * density)

def rounded(inputs):
    return lax.optimization_barrier(inputs.astype(jnp.bfloat16)).astype(jnp.float32)

def reference(layer_in, cotangent, norm1_gain, norm1_shift, norm2_gain, norm2_shift, qkv_weight, qv_bias, key_bias, attn_out_weight, attn_out_bias, ff_in_weight, ff_in_bias, ff_out_weight, ff_out_bias):
    length = LENGTH
    qblock = math.gcd(length, 512)
    nblocks = length // qblock
    positions = paired_position(jnp.arange(length, dtype=jnp.int32), BLK, N_CTX)
    cosine, sine = rotary_tables(positions)
    gain_one = norm1_gain.astype(jnp.float32)
    shift_one = norm1_shift.astype(jnp.float32)
    gain_two = norm2_gain.astype(jnp.float32)
    shift_two = norm2_shift.astype(jnp.float32)
    key_full = jnp.concatenate([key_bias.astype(jnp.float32).reshape(H, ROT), jnp.zeros((H, HD - ROT), jnp.float32)], axis=1).reshape(D)
    in_bias = jnp.concatenate([qv_bias[:D].astype(jnp.float32), key_full, qv_bias[D:].astype(jnp.float32)])
    ff_bias = ff_in_bias.astype(jnp.float32)
    attn_bias = attn_out_bias.astype(jnp.float32)
    out_bias = ff_out_bias.astype(jnp.float32)

    def sequence(totals, inputs):
        tokens_in, upstream = inputs
        inputs_f = tokens_in.astype(jnp.float32)
        upstream_f = upstream.astype(jnp.float32)
        normed_one, unit_one, inverse_one = layer_norm(inputs_f, gain_one, shift_one)
        normed_two, unit_two, inverse_two = layer_norm(inputs_f, gain_two, shift_two)
        one_b = normed_one.astype(jnp.bfloat16)
        two_b = normed_two.astype(jnp.bfloat16)
        projected = jnp.dot(one_b, qkv_weight, preferred_element_type=jnp.float32) + in_bias
        ff_pre = jnp.dot(two_b, ff_in_weight, preferred_element_type=jnp.float32) + ff_bias
        query_b = rotate(projected[:, :D].reshape(length, H, HD), cosine, sine).astype(jnp.bfloat16)
        keys_b = rotate(projected[:, D:2 * D].reshape(length, H, HD), cosine, sine).astype(jnp.bfloat16)
        values_b = projected[:, 2 * D:].reshape(length, H, HD).astype(jnp.bfloat16)
        query_f = query_b.astype(jnp.float32)
        keys_f = keys_b.astype(jnp.float32)
        values_f = values_b.astype(jnp.float32)

        def scores_for(number):
            start = number * qblock
            rows_q = lax.dynamic_slice_in_dim(query_f, start, qblock, 0)
            pos_q = lax.dynamic_slice_in_dim(positions, start, qblock, 0)
            scores = jnp.einsum('qhd,khd->hqk', rows_q, keys_f) * 0.125
            allowed = positions[None, None, :] <= pos_q[None, :, None]
            return (jnp.where(allowed, scores, -1e+30), allowed, rows_q)

        def attend(number):
            scores, allowed, rows_q = scores_for(number)
            highest = lax.optimization_barrier(jnp.max(scores, axis=-1, keepdims=True))
            log_total = highest + jnp.log(lax.optimization_barrier(jnp.sum(jnp.exp(scores - highest), axis=-1, keepdims=True)))
            weights = jnp.where(allowed, jnp.exp(scores - log_total), 0.0)
            mixed = jnp.einsum('hqk,khd->qhd', rounded(weights), values_f)
            return (mixed, log_total[..., 0])
        mixed, log_totals = lax.map(attend, jnp.arange(nblocks, dtype=jnp.int32))
        attn_b = mixed.reshape(length, D).astype(jnp.bfloat16)
        activation, slope = gelu_parts(ff_pre)
        gelu_b = activation.astype(jnp.bfloat16)
        mixture = jnp.dot(attn_b, attn_out_weight.T, preferred_element_type=jnp.float32) + jnp.dot(gelu_b, ff_out_weight.T, preferred_element_type=jnp.float32)
        result = (inputs_f + mixture + attn_bias + out_bias).astype(jnp.bfloat16)
        dout_b = jnp.dot(upstream, attn_out_weight, preferred_element_type=jnp.float32).astype(jnp.bfloat16)
        dgelu = jnp.dot(upstream, ff_out_weight, preferred_element_type=jnp.float32)
        dpre = dgelu * slope
        dpre_b = dpre.astype(jnp.bfloat16)
        dout_f = dout_b.astype(jnp.float32).reshape(length, H, HD)
        delta = lax.optimization_barrier(jnp.sum(dout_f * attn_b.astype(jnp.float32).reshape(length, H, HD), axis=-1)).T

        def attend_back(sums, number):
            key_sum, value_sum = sums
            scores, allowed, rows_q = scores_for(number)
            start = number * qblock
            rows_do = lax.dynamic_slice_in_dim(dout_f, start, qblock, 0)
            rows_delta = lax.dynamic_slice_in_dim(delta, start, qblock, 1)
            rows_lse = log_totals[number]
            probs = jnp.where(allowed, jnp.exp(scores - rows_lse[..., None]), 0.0)
            dprobs = jnp.einsum('qhd,khd->hqk', rows_do, values_f)
            dscores = rounded(probs * (dprobs - rows_delta[..., None]))
            dquery = jnp.einsum('hqk,khd->qhd', dscores, keys_f) * 0.125
            key_sum = key_sum + jnp.einsum('hqk,qhd->khd', dscores, rows_q) * 0.125
            value_sum = value_sum + jnp.einsum('hqk,qhd->khd', rounded(probs), rows_do)
            return ((key_sum, value_sum), dquery)
        zero_heads = jnp.zeros((length, H, HD), jnp.float32)
        (dkeys, dvalues), dqueries = lax.scan(attend_back, (zero_heads, zero_heads), jnp.arange(nblocks, dtype=jnp.int32))
        dquery_pre = rotate_back(dqueries.reshape(length, H, HD), cosine, sine)
        dkey_pre = rotate_back(dkeys, cosine, sine)
        dproj = jnp.concatenate([dquery_pre.reshape(length, D), dkey_pre.reshape(length, D), dvalues.reshape(length, D)], axis=1)
        dproj_b = dproj.astype(jnp.bfloat16)
        dnormed_one = jnp.dot(dproj_b, qkv_weight.T, preferred_element_type=jnp.float32)
        dnormed_two = jnp.dot(dpre_b, ff_in_weight.T, preferred_element_type=jnp.float32)
        dinput_one, gain_grad_one, shift_grad_one = norm_back(dnormed_one, unit_one, inverse_one, gain_one)
        dinput_two, gain_grad_two, shift_grad_two = norm_back(dnormed_two, unit_two, inverse_two, gain_two)
        dinput = upstream_f + dinput_one + dinput_two
        cot_sum = lax.optimization_barrier(jnp.sum(upstream_f, axis=0))
        grads = (gain_grad_one, shift_grad_one, gain_grad_two, shift_grad_two, jnp.dot(one_b.T, dproj_b, preferred_element_type=jnp.float32), jnp.concatenate([lax.optimization_barrier(jnp.sum(dquery_pre.reshape(length, D), axis=0)), lax.optimization_barrier(jnp.sum(dvalues.reshape(length, D), axis=0))]), lax.optimization_barrier(jnp.sum(dkey_pre[:, :, :ROT], axis=0)).reshape(H * ROT), jnp.dot(upstream.T, attn_b, preferred_element_type=jnp.float32), cot_sum, jnp.dot(two_b.T, dpre_b, preferred_element_type=jnp.float32), lax.optimization_barrier(jnp.sum(dpre, axis=0)), jnp.dot(upstream.T, gelu_b, preferred_element_type=jnp.float32), cot_sum)
        totals = jax.tree.map(jnp.add, totals, grads)
        return (totals, (result, dinput))
    zero_totals = (jnp.zeros((D,), jnp.float32), jnp.zeros((D,), jnp.float32), jnp.zeros((D,), jnp.float32), jnp.zeros((D,), jnp.float32), jnp.zeros((D, 3 * D), jnp.float32), jnp.zeros((2 * D,), jnp.float32), jnp.zeros((H * ROT,), jnp.float32), jnp.zeros((D, D), jnp.float32), jnp.zeros((D,), jnp.float32), jnp.zeros((D, FF), jnp.float32), jnp.zeros((FF,), jnp.float32), jnp.zeros((D, FF), jnp.float32), jnp.zeros((D,), jnp.float32))
    totals, (layer_out, input_grad) = lax.scan(sequence, zero_totals, (layer_in, cotangent))
    return (layer_out, input_grad, totals[0], totals[1], totals[2], totals[3], totals[4], totals[5], totals[6], totals[7], totals[8], totals[9], totals[10], totals[11], totals[12])
```

```python
import math

import jax
import jax.numpy as jnp
from jax import lax
from jax.experimental import pallas as pl
from jax.experimental.pallas import tpu as pltpu
from jax.sharding import PartitionSpec as P

D = 1024
H = 16
HD = 64
ROT = 16


EPSILON = 1e-05


def gelu_parts(inputs):
    cumulative = 0.5 * (1.0 + lax.erf(inputs * (1.0 / math.sqrt(2.0))))
    density = jnp.exp(-0.5 * inputs * inputs) * (1.0 / math.sqrt(2.0 * math.pi))
    return (inputs * cumulative, cumulative + inputs * density)


def rows_dot(left, right):
    return lax.dot_general(
        left, right, (((0,), (0,)), ((), ())), preferred_element_type=jnp.float32
    )


def cols_dot(left, right):
    return lax.dot_general(
        left, right, (((1,), (1,)), ((), ())), preferred_element_type=jnp.float32
    )


def rotary_wide(positions, width):
    halfway = ROT // 2
    lane = jnp.arange(width, dtype=jnp.int32) % HD
    step = (lane % halfway).astype(jnp.float32)
    frequency = jnp.exp(step * (-2.0 * math.log(10000.0) / ROT))
    theta = positions.astype(jnp.float32)[:, None] * frequency[None, :]
    cosine = jnp.where(lane < ROT, jnp.cos(theta), 1.0)
    sine = jnp.sin(theta)
    low = jnp.where(lane < halfway, sine, 0.0)
    high = jnp.where((lane >= halfway) & (lane < ROT), sine, 0.0)
    return cosine, low, high


def shifted(inputs, amount):
    return jnp.roll(inputs, -amount, axis=-1)


def attention_kernel(q_ref, k_ref, v_ref, do_ref, o_ref, dq_ref, dk_ref, dv_ref, ds_s, pw_s):
    groups = q_ref.shape[0]
    tokens = q_ref.shape[2]
    half = tokens // 2
    width = q_ref.shape[3]
    length = groups * tokens
    tile = min(256, length)

    def natural(ref, lanes):
        pieces = [ref[c, 0, 0:half, lanes] for c in range(groups)]
        pieces += [ref[c, 0, half:tokens, lanes] for c in reversed(range(groups))]
        return jnp.concatenate(pieces, axis=0)

    def put(ref, lanes, first, values):
        for i in range(values.shape[0] // half):
            b = first // half + i
            piece = values[i * half : (i + 1) * half].astype(ref.dtype)
            if b < groups:
                ref[b, 0, 0:half, lanes] = piece
            else:
                ref[2 * groups - 1 - b, 0, half:tokens, lanes] = piece

    for head in range(width // HD):
        lanes = slice(head * HD, (head + 1) * HD)
        q = natural(q_ref, lanes)
        k = natural(k_ref, lanes)
        v = natural(v_ref, lanes)
        do = natural(do_ref, lanes)
        row = lax.broadcasted_iota(jnp.int32, (tile, tile), 0)
        col = lax.broadcasted_iota(jnp.int32, (tile, tile), 1)
        allowed = col <= row
        for i in range(length // tile):
            start = i * tile
            stop = start + tile
            q_i = q[start:stop]
            do_i = do[start:stop]
            scores = cols_dot(q_i, k[:stop]) * 0.125
            diag = jnp.where(allowed, scores[:, start:stop], -1e30)
            scores = jnp.concatenate([scores[:, :start], diag], axis=1) if start else diag
            highest = jnp.max(scores, axis=-1, keepdims=True)
            powers = jnp.exp(scores - highest)
            total = jnp.sum(powers, axis=-1, keepdims=True)
            probs = powers * (1.0 / total)
            weights = probs.astype(jnp.bfloat16)
            mixed = jnp.dot(weights, v[:stop], preferred_element_type=jnp.float32)
            mixed_b = mixed.astype(jnp.bfloat16)
            delta = jnp.sum(
                do_i.astype(jnp.float32) * mixed_b.astype(jnp.float32), axis=-1, keepdims=True
            )
            dprobs = cols_dot(do_i, v[:stop])
            dscores = (probs * (dprobs - delta)).astype(jnp.bfloat16)
            dq = jnp.dot(dscores, k[:stop], preferred_element_type=jnp.float32) * 0.125
            put(o_ref, lanes, start, mixed_b)
            put(dq_ref, lanes, start, dq)
            pw_s[start:stop, :stop] = weights
            ds_s[start:stop, :stop] = dscores
        for j in range(length // tile):
            start = j * tile
            stop = start + tile
            dk = rows_dot(ds_s[start:, start:stop], q[start:]) * 0.125
            dv = rows_dot(pw_s[start:, start:stop], do[start:])
            put(dk_ref, lanes, start, dk)
            put(dv_ref, lanes, start, dv)


def attention(q, k, v, do):
    groups, seqs, tokens, width = q.shape
    length = groups * tokens
    spec = pl.BlockSpec((groups, 1, tokens, width), lambda i: (0, i, 0, 0))
    shape = (groups, seqs, tokens, width)
    return pl.pallas_call(
        attention_kernel,
        grid=(seqs,),
        in_specs=[spec] * 4,
        out_specs=[spec] * 4,
        out_shape=[jax.ShapeDtypeStruct(shape, jnp.bfloat16)]
        + [jax.ShapeDtypeStruct(shape, jnp.float32)] * 3,
        scratch_shapes=[pltpu.VMEM((length, length), jnp.bfloat16)] * 2,
        compiler_params=pltpu.CompilerParams(vmem_limit_bytes=50 * 1024 * 1024),
        name="attention",
    )(q, k, v, do)


def per_device(
    layer_in,
    cotangent,
    norm1_gain,
    norm1_shift,
    norm2_gain,
    norm2_shift,
    qkv_weight,
    qv_bias,
    key_bias,
    attn_out_weight,
    attn_out_bias,
    ff_in_weight,
    ff_in_bias,
    ff_out_weight,
    ff_out_bias,
):
    groups = lax.axis_size("ctx")
    shards = lax.axis_size("fsdp")
    place = lax.axis_index("ctx")
    seqs, tokens = layer_in.shape[:2]
    half = tokens // 2
    rows = groups * seqs * tokens
    wide = D // groups
    hidden = ff_in_weight.shape[1] // groups
    share = D // shards
    cut = lambda m, base, n: lax.dynamic_slice_in_dim(m, base + place * n, n, m.ndim - 1)

    small = (
        norm1_gain, norm1_shift, norm2_gain, norm2_shift,
        qv_bias, key_bias, attn_out_bias, ff_in_bias, ff_out_bias,
    )
    packed = jnp.concatenate(small)
    extra = -(-packed.shape[0] // (4 * wide * 16)) * 16
    packed = jnp.pad(packed, (0, extra * 4 * wide - packed.shape[0])).reshape(extra, 4 * wide)
    attn_cols = jnp.concatenate(
        [cut(qkv_weight, 0, wide), cut(qkv_weight, D, wide), cut(qkv_weight, 2 * D, wide),
         cut(attn_out_weight, 0, wide)], axis=1)
    attn_cols = jnp.concatenate([attn_cols, packed], axis=0)
    ff_cols = jnp.concatenate([cut(ff_in_weight, 0, hidden), cut(ff_out_weight, 0, hidden)], axis=1)
    x_all = lax.all_gather(layer_in, "ctx", axis=0)
    attn_full = lax.all_gather(attn_cols, "fsdp", axis=0)
    dy_all = lax.all_gather(cotangent, "ctx", axis=0)
    ff_full = lax.all_gather(ff_cols, "fsdp", axis=0, tiled=True)
    flat = attn_full[:, share:].reshape(shards, extra * 4 * wide).astype(jnp.float32)
    vectors = []
    start = 0
    for piece in small:
        n = piece.shape[0]
        vectors.append(flat[:, start : start + n].reshape(shards * n))
        start += n
    gain_one, shift_one, gain_two, shift_two, qv_all, key_all, attn_bias, ff_bias, out_bias = vectors
    attn_full = attn_full[:, :share].reshape(D, 4 * wide)
    qkv_w, ao_w = attn_full[:, : 3 * wide], attn_full[:, 3 * wide :]
    fi_w, fo_w = ff_full[:, :hidden], ff_full[:, hidden:]
    key_bias_full = jnp.pad(key_all.reshape(H, ROT), ((0, 0), (0, HD - ROT))).reshape(D)
    in_bias = jnp.concatenate(
        [cut(qv_all, 0, wide), cut(key_bias_full, 0, wide), cut(qv_all, D, wide)])
    ff_bias_own = cut(ff_bias, 0, hidden)

    x = x_all.reshape(rows, D).astype(jnp.float32)
    dy = dy_all.reshape(rows, D)
    average = jnp.mean(x, axis=-1, keepdims=True)
    centred = x - average
    inverse = lax.rsqrt(jnp.mean(centred * centred, axis=-1, keepdims=True) + EPSILON)
    unit = centred * inverse
    one_b = (unit * gain_one + shift_one).astype(jnp.bfloat16)
    two_b = (unit * gain_two + shift_two).astype(jnp.bfloat16)

    device_of = jnp.arange(groups, dtype=jnp.int32)[:, None]
    within = jnp.arange(tokens, dtype=jnp.int32)[None, :]
    pos = jnp.where(
        within < half,
        device_of * half + within,
        2 * half * groups - (device_of + 2) * half + within,
    ).reshape(groups * tokens)
    cosine, low, high = [
        t.reshape(groups, 1, tokens, 2 * wide) for t in rotary_wide(pos, 2 * wide)]
    projected = jnp.dot(one_b, qkv_w, preferred_element_type=jnp.float32) + in_bias
    projected = projected.reshape(groups, seqs, tokens, 3 * wide)
    qk = projected[..., : 2 * wide]
    halfway = ROT // 2
    qk = (qk * cosine - shifted(qk, halfway) * low + shifted(qk, -halfway) * high).astype(
        jnp.bfloat16)
    values = projected[..., 2 * wide :].astype(jnp.bfloat16)
    dout = jnp.dot(dy, ao_w, preferred_element_type=jnp.float32).astype(jnp.bfloat16)
    dout = dout.reshape(groups, seqs, tokens, wide)
    mixed, dq, dk, dv = attention(qk[..., :wide], qk[..., wide:], values, dout)
    dqk = jnp.concatenate([dq, dk], axis=-1)
    dqk = dqk * cosine + shifted(dqk, halfway) * low - shifted(dqk, -halfway) * high
    dproj = jnp.concatenate([dqk, dv], axis=-1).reshape(rows, 3 * wide)
    dproj_b = dproj.astype(jnp.bfloat16)

    hpre = jnp.dot(two_b, fi_w, preferred_element_type=jnp.float32) + ff_bias_own
    activation, slope = gelu_parts(hpre)
    gelu_b = activation.astype(jnp.bfloat16)
    dpre = jnp.dot(dy, fo_w, preferred_element_type=jnp.float32) * slope
    dpre_b = dpre.astype(jnp.bfloat16)
    ff_terms = jnp.concatenate([rows_dot(two_b, dpre_b), rows_dot(dy, gelu_b)], axis=1)
    ff_own = lax.psum_scatter(
        ff_terms.astype(jnp.bfloat16), "fsdp", scatter_dimension=0, tiled=True)

    mixed = mixed.reshape(rows, wide)
    out_part = cols_dot(mixed, ao_w) + cols_dot(gelu_b, fo_w)
    out_sum = lax.psum_scatter(
        out_part.astype(jnp.bfloat16).reshape(groups, seqs, tokens, D), "ctx", scatter_dimension=0)
    layer_out = (
        layer_in.astype(jnp.float32) + out_sum.astype(jnp.float32) + attn_bias + out_bias
    ).astype(jnp.bfloat16)

    dn_one = cols_dot(dproj_b, qkv_w)
    dn_two = cols_dot(dpre_b, fi_w)
    scaled_part = (dn_one * gain_one + dn_two * gain_two).astype(jnp.bfloat16)
    scaled = lax.psum_scatter(
        scaled_part.reshape(groups, seqs, tokens, D), "ctx", scatter_dimension=0
    ).astype(jnp.float32)
    x_own = layer_in.astype(jnp.float32)
    mean_own = jnp.mean(x_own, axis=-1, keepdims=True)
    centred_own = x_own - mean_own
    inverse_own = lax.rsqrt(jnp.mean(centred_own * centred_own, axis=-1, keepdims=True) + EPSILON)
    unit_own = centred_own * inverse_own
    input_grad = cotangent.astype(jnp.float32) + inverse_own * (
        scaled
        - jnp.mean(scaled, axis=-1, keepdims=True)
        - unit_own * jnp.mean(scaled * unit_own, axis=-1, keepdims=True)
    )

    def spread(vector, total, base):
        whole = lax.dynamic_update_slice_in_dim(
            jnp.zeros((total,), jnp.float32), vector, base + place * vector.shape[0], 0)
        return whole.reshape(shards, total // shards)

    colsum = jnp.sum(dproj, axis=0)
    key_cols = colsum[wide : 2 * wide].reshape(wide // HD, HD)[:, :ROT].reshape(-1)
    pieces = [
        jnp.sum(dn_one * unit, axis=0).reshape(shards, share),
        jnp.sum(dn_one, axis=0).reshape(shards, share),
        jnp.sum(dn_two * unit, axis=0).reshape(shards, share),
        jnp.sum(dn_two, axis=0).reshape(shards, share),
        spread(colsum[:wide], 2 * D, 0) + spread(colsum[2 * wide :], 2 * D, D),
        spread(key_cols, H * ROT, 0),
        jnp.sum(cotangent.astype(jnp.float32), axis=(0, 1)).reshape(shards, share),
        spread(jnp.sum(dpre, axis=0), hidden * groups, 0),
    ]
    packed_grads = jnp.concatenate(pieces, axis=1)
    used = packed_grads.shape[1]
    more = -(-used // (4 * wide * 16)) * 16
    packed_grads = jnp.pad(packed_grads, ((0, 0), (0, more * 4 * wide - used)))
    attn_terms = jnp.concatenate([rows_dot(one_b, dproj_b), rows_dot(dy, mixed)], axis=1)
    attn_terms = jnp.concatenate(
        [attn_terms.reshape(shards, share, 4 * wide), packed_grads.reshape(shards, more, 4 * wide)],
        axis=1)
    attn_own = lax.psum_scatter(attn_terms.astype(jnp.bfloat16), "fsdp", scatter_dimension=0)
    ff_grads = lax.all_gather(ff_own, "ctx", axis=0)
    attn_grads = lax.all_gather(attn_own, "ctx", axis=0)

    def side_by_side(stacked):
        return stacked.transpose(1, 0, 2).reshape(share, -1).astype(jnp.float32)

    matrices = attn_grads[:, :share]
    qkv_grad = jnp.concatenate(
        [side_by_side(matrices[..., i * wide : (i + 1) * wide]) for i in range(3)], axis=1)
    ao_grad = side_by_side(matrices[..., 3 * wide :])
    fi_grad = side_by_side(ff_grads[..., :hidden])
    fo_grad = side_by_side(ff_grads[..., hidden:])
    vec = jnp.sum(attn_grads[:, share:].astype(jnp.float32), axis=0).reshape(-1)
    shares = []
    start = 0
    for piece in pieces:
        shares.append(vec[start : start + piece.shape[1]])
        start += piece.shape[1]
    return (
        layer_out,
        input_grad,
        shares[0],
        shares[1],
        shares[2],
        shares[3],
        qkv_grad,
        shares[4],
        shares[5],
        ao_grad,
        shares[6],
        fi_grad,
        shares[7],
        fo_grad,
        shares[6],
    )


def solution(mesh):
    placed = (
        P("fsdp", "ctx", None),
        P("fsdp", "ctx", None),
        P("fsdp"),
        P("fsdp"),
        P("fsdp"),
        P("fsdp"),
        P("fsdp", None),
        P("fsdp"),
        P("fsdp"),
        P("fsdp", None),
        P("fsdp"),
        P("fsdp", None),
        P("fsdp"),
        P("fsdp", None),
        P("fsdp"),
    )
    return jax.shard_map(
        per_device,
        mesh=mesh,
        in_specs=placed,
        out_specs=(
            P("fsdp", "ctx", None),
            P("fsdp", "ctx", None),
            P("fsdp"),
            P("fsdp"),
            P("fsdp"),
            P("fsdp"),
            P("fsdp", None),
            P("fsdp"),
            P("fsdp"),
            P("fsdp", None),
            P("fsdp"),
            P("fsdp", None),
            P("fsdp"),
            P("fsdp", None),
            P("fsdp"),
        ),
        check_vma=False,
    )
```

```python
import math

import jax
import jax.numpy as jnp
from jax import lax
from jax.experimental import pallas as pl
from jax.experimental.pallas import tpu as pltpu
from jax.sharding import PartitionSpec as P

D = 1024
H = 16
HD = 64
ROT = 16


EPSILON = 1e-05


def gelu_parts(inputs):
    cumulative = 0.5 * (1.0 + lax.erf(inputs * (1.0 / math.sqrt(2.0))))
    density = jnp.exp(-0.5 * inputs * inputs) * (1.0 / math.sqrt(2.0 * math.pi))
    return (inputs * cumulative, cumulative + inputs * density)


def rows_dot(left, right):
    return lax.dot_general(
        left, right, (((0,), (0,)), ((), ())), preferred_element_type=jnp.float32
    )


def cols_dot(left, right):
    return lax.dot_general(
        left, right, (((1,), (1,)), ((), ())), preferred_element_type=jnp.float32
    )


def rotary_wide(positions, width):
    halfway = ROT // 2
    lane = jnp.arange(width, dtype=jnp.int32) % HD
    step = (lane % halfway).astype(jnp.float32)
    frequency = jnp.exp(step * (-2.0 * math.log(10000.0) / ROT))
    theta = positions.astype(jnp.float32)[:, None] * frequency[None, :]
    cosine = jnp.where(lane < ROT, jnp.cos(theta), 1.0)
    sine = jnp.sin(theta)
    low = jnp.where(lane < halfway, sine, 0.0)
    high = jnp.where((lane >= halfway) & (lane < ROT), sine, 0.0)
    return cosine, low, high


def shifted(inputs, amount):
    return jnp.roll(inputs, -amount, axis=-1)


def attention_kernel(q_ref, k_ref, v_ref, do_ref, o_ref, dq_ref, dk_ref, dv_ref, ds_s, pw_s):
    groups = q_ref.shape[0]
    tokens = q_ref.shape[2]
    half = tokens // 2
    width = q_ref.shape[3]
    length = groups * tokens
    tile = min(256, length)

    def natural(ref, lanes):
        pieces = [ref[c, 0, 0:half, lanes] for c in range(groups)]
        pieces += [ref[c, 0, half:tokens, lanes] for c in reversed(range(groups))]
        return jnp.concatenate(pieces, axis=0)

    def put(ref, lanes, first, values):
        for i in range(values.shape[0] // half):
            b = first // half + i
            piece = values[i * half : (i + 1) * half].astype(ref.dtype)
            if b < groups:
                ref[b, 0, 0:half, lanes] = piece
            else:
                ref[2 * groups - 1 - b, 0, half:tokens, lanes] = piece

    for head in range(width // HD):
        lanes = slice(head * HD, (head + 1) * HD)
        q = natural(q_ref, lanes)
        k = natural(k_ref, lanes)
        v = natural(v_ref, lanes)
        do = natural(do_ref, lanes)
        row = lax.broadcasted_iota(jnp.int32, (tile, tile), 0)
        col = lax.broadcasted_iota(jnp.int32, (tile, tile), 1)
        allowed = col <= row
        for i in range(length // tile):
            start = i * tile
            stop = start + tile
            q_i = q[start:stop]
            do_i = do[start:stop]
            scores = cols_dot(q_i, k[:stop]) * 0.125
            diag = jnp.where(allowed, scores[:, start:stop], -1e30)
            scores = jnp.concatenate([scores[:, :start], diag], axis=1) if start else diag
            highest = jnp.max(scores, axis=-1, keepdims=True)
            powers = jnp.exp(scores - highest)
            total = jnp.sum(powers, axis=-1, keepdims=True)
            probs = powers * (1.0 / total)
            weights = probs.astype(jnp.bfloat16)
            mixed = jnp.dot(weights, v[:stop], preferred_element_type=jnp.float32)
            mixed_b = mixed.astype(jnp.bfloat16)
            delta = jnp.sum(
                do_i.astype(jnp.float32) * mixed_b.astype(jnp.float32), axis=-1, keepdims=True
            )
            dprobs = cols_dot(do_i, v[:stop])
            dscores = (probs * (dprobs - delta)).astype(jnp.bfloat16)
            dq = jnp.dot(dscores, k[:stop], preferred_element_type=jnp.float32) * 0.125
            put(o_ref, lanes, start, mixed_b)
            put(dq_ref, lanes, start, dq)
            pw_s[start:stop, :stop] = weights
            ds_s[start:stop, :stop] = dscores
        for j in range(length // tile):
            start = j * tile
            stop = start + tile
            dk = rows_dot(ds_s[start:, start:stop], q[start:]) * 0.125
            dv = rows_dot(pw_s[start:, start:stop], do[start:])
            put(dk_ref, lanes, start, dk)
            put(dv_ref, lanes, start, dv)


def attention(q, k, v, do):
    groups, seqs, tokens, width = q.shape
    length = groups * tokens
    spec = pl.BlockSpec((groups, 1, tokens, width), lambda i: (0, i, 0, 0))
    shape = (groups, seqs, tokens, width)
    return pl.pallas_call(
        attention_kernel,
        grid=(seqs,),
        in_specs=[spec] * 4,
        out_specs=[spec] * 4,
        out_shape=[jax.ShapeDtypeStruct(shape, jnp.bfloat16)]
        + [jax.ShapeDtypeStruct(shape, jnp.float32)] * 3,
        scratch_shapes=[pltpu.VMEM((length, length), jnp.bfloat16)] * 2,
        compiler_params=pltpu.CompilerParams(vmem_limit_bytes=50 * 1024 * 1024),
        name="attention",
    )(q, k, v, do)


def gather_blocks(shard):
    count = lax.axis_size("fsdp")
    own = lax.axis_index("fsdp")
    stacked = jnp.zeros((count,) + shard.shape, shard.dtype)
    for step in range(count):
        ring = [(j, (j + step) % count) for j in range(count)]
        piece = lax.ppermute(shard, "fsdp", ring) if step else shard
        stacked = lax.dynamic_update_index_in_dim(stacked, piece, (own - step) % count, 0)
    return stacked


def scatter_blocks(terms):
    count = lax.axis_size("fsdp")
    own = lax.axis_index("fsdp")
    total = lax.dynamic_index_in_dim(terms, own, 0, keepdims=False).astype(jnp.float32)
    for step in range(1, count):
        ring = [(j, (j + step) % count) for j in range(count)]
        block = lax.dynamic_index_in_dim(terms, (own + step) % count, 0, keepdims=False)
        total = total + lax.ppermute(block, "fsdp", ring).astype(jnp.float32)
    return total.astype(jnp.bfloat16)


def column_kernel(in_ref, out_ref):
    out_ref[...] = in_ref[0].astype(jnp.float32)


def columns(stacked, share, first, width, parts):
    groups = stacked.shape[0]
    if width % 128:
        pieces = []
        for p in range(parts):
            piece = stacked[:, :share, first + p * width : first + (p + 1) * width]
            pieces.append(piece.transpose(1, 0, 2).reshape(share, -1))
        return jnp.concatenate(pieces, axis=1).astype(jnp.float32)
    return pl.pallas_call(
        column_kernel,
        grid=(parts, groups),
        in_specs=[pl.BlockSpec((1, share, width), lambda p, c: (c, 0, first // width + p))],
        out_specs=pl.BlockSpec((share, width), lambda p, c: (0, p * groups + c)),
        out_shape=jax.ShapeDtypeStruct((share, parts * groups * width), jnp.float32),
        name="columns",
    )(stacked)


def per_device(
    layer_in,
    cotangent,
    norm1_gain,
    norm1_shift,
    norm2_gain,
    norm2_shift,
    qkv_weight,
    qv_bias,
    key_bias,
    attn_out_weight,
    attn_out_bias,
    ff_in_weight,
    ff_in_bias,
    ff_out_weight,
    ff_out_bias,
):
    groups = lax.axis_size("ctx")
    shards = lax.axis_size("fsdp")
    place = lax.axis_index("ctx")
    seqs, tokens = layer_in.shape[:2]
    half = tokens // 2
    rows = groups * seqs * tokens
    wide = D // groups
    hidden = ff_in_weight.shape[1] // groups
    share = D // shards
    cut = lambda m, base, n: lax.dynamic_slice_in_dim(m, base + place * n, n, m.ndim - 1)

    small = (
        norm1_gain, norm1_shift, norm2_gain, norm2_shift,
        qv_bias, key_bias, attn_out_bias, ff_in_bias, ff_out_bias,
    )
    packed = jnp.concatenate(small)
    extra = -(-packed.shape[0] // (4 * wide * 16)) * 16
    packed = jnp.pad(packed, (0, extra * 4 * wide - packed.shape[0])).reshape(extra, 4 * wide)
    attn_cols = jnp.concatenate(
        [cut(qkv_weight, 0, wide), cut(qkv_weight, D, wide), cut(qkv_weight, 2 * D, wide),
         cut(attn_out_weight, 0, wide)], axis=1)
    attn_cols = jnp.concatenate([attn_cols, packed], axis=0)
    ff_cols = jnp.concatenate([cut(ff_in_weight, 0, hidden), cut(ff_out_weight, 0, hidden)], axis=1)
    x_all = lax.all_gather(layer_in, "ctx", axis=0)
    attn_full = gather_blocks(attn_cols)
    dy_all = lax.all_gather(cotangent, "ctx", axis=0)
    ff_full = gather_blocks(ff_cols).reshape(D, 2 * hidden)
    flat = attn_full[:, share:].reshape(shards, extra * 4 * wide).astype(jnp.float32)
    vectors = []
    start = 0
    for piece in small:
        n = piece.shape[0]
        vectors.append(flat[:, start : start + n].reshape(shards * n))
        start += n
    gain_one, shift_one, gain_two, shift_two, qv_all, key_all, attn_bias, ff_bias, out_bias = vectors
    attn_full = attn_full[:, :share].reshape(D, 4 * wide)
    qkv_w, ao_w = attn_full[:, : 3 * wide], attn_full[:, 3 * wide :]
    fi_w, fo_w = ff_full[:, :hidden], ff_full[:, hidden:]
    key_bias_full = jnp.pad(key_all.reshape(H, ROT), ((0, 0), (0, HD - ROT))).reshape(D)
    in_bias = jnp.concatenate(
        [cut(qv_all, 0, wide), cut(key_bias_full, 0, wide), cut(qv_all, D, wide)])
    ff_bias_own = cut(ff_bias, 0, hidden)

    x = x_all.reshape(rows, D).astype(jnp.float32)
    dy = dy_all.reshape(rows, D)
    average = jnp.mean(x, axis=-1, keepdims=True)
    centred = x - average
    inverse = lax.rsqrt(jnp.mean(centred * centred, axis=-1, keepdims=True) + EPSILON)
    unit = centred * inverse
    one_b = (unit * gain_one + shift_one).astype(jnp.bfloat16)
    two_b = (unit * gain_two + shift_two).astype(jnp.bfloat16)

    device_of = jnp.arange(groups, dtype=jnp.int32)[:, None]
    within = jnp.arange(tokens, dtype=jnp.int32)[None, :]
    pos = jnp.where(
        within < half,
        device_of * half + within,
        2 * half * groups - (device_of + 2) * half + within,
    ).reshape(groups * tokens)
    cosine, low, high = [
        t.reshape(groups, 1, tokens, 2 * wide) for t in rotary_wide(pos, 2 * wide)]
    projected = jnp.dot(one_b, qkv_w, preferred_element_type=jnp.float32) + in_bias
    projected = projected.reshape(groups, seqs, tokens, 3 * wide)
    qk = projected[..., : 2 * wide]
    halfway = ROT // 2
    qk = (qk * cosine - shifted(qk, halfway) * low + shifted(qk, -halfway) * high).astype(
        jnp.bfloat16)
    values = projected[..., 2 * wide :].astype(jnp.bfloat16)
    dout = jnp.dot(dy, ao_w, preferred_element_type=jnp.float32).astype(jnp.bfloat16)
    dout = dout.reshape(groups, seqs, tokens, wide)
    mixed, dq, dk, dv = attention(qk[..., :wide], qk[..., wide:], values, dout)
    dqk = jnp.concatenate([dq, dk], axis=-1)
    dqk = dqk * cosine + shifted(dqk, halfway) * low - shifted(dqk, -halfway) * high
    dproj = jnp.concatenate([dqk, dv], axis=-1).reshape(rows, 3 * wide)
    dproj_b = dproj.astype(jnp.bfloat16)

    hpre = jnp.dot(two_b, fi_w, preferred_element_type=jnp.float32) + ff_bias_own
    activation, slope = gelu_parts(hpre)
    gelu_b = activation.astype(jnp.bfloat16)
    dpre = jnp.dot(dy, fo_w, preferred_element_type=jnp.float32) * slope
    dpre_b = dpre.astype(jnp.bfloat16)
    ff_terms = jnp.concatenate([rows_dot(two_b, dpre_b), rows_dot(dy, gelu_b)], axis=1)
    ff_own = scatter_blocks(
        ff_terms.astype(jnp.bfloat16).reshape(shards, share, 2 * hidden))

    mixed = mixed.reshape(rows, wide)
    out_part = cols_dot(mixed, ao_w) + cols_dot(gelu_b, fo_w)
    out_sum = lax.psum_scatter(
        out_part.astype(jnp.bfloat16).reshape(groups, seqs, tokens, D), "ctx", scatter_dimension=0)
    layer_out = (
        layer_in.astype(jnp.float32) + out_sum.astype(jnp.float32) + attn_bias + out_bias
    ).astype(jnp.bfloat16)

    dn_one = cols_dot(dproj_b, qkv_w)
    dn_two = cols_dot(dpre_b, fi_w)
    scaled_part = (dn_one * gain_one + dn_two * gain_two).astype(jnp.bfloat16)
    scaled = lax.psum_scatter(
        scaled_part.reshape(groups, seqs, tokens, D), "ctx", scatter_dimension=0
    ).astype(jnp.float32)
    x_own = layer_in.astype(jnp.float32)
    mean_own = jnp.mean(x_own, axis=-1, keepdims=True)
    centred_own = x_own - mean_own
    inverse_own = lax.rsqrt(jnp.mean(centred_own * centred_own, axis=-1, keepdims=True) + EPSILON)
    unit_own = centred_own * inverse_own
    input_grad = cotangent.astype(jnp.float32) + inverse_own * (
        scaled
        - jnp.mean(scaled, axis=-1, keepdims=True)
        - unit_own * jnp.mean(scaled * unit_own, axis=-1, keepdims=True)
    )

    def spread(vector, total, base):
        whole = lax.dynamic_update_slice_in_dim(
            jnp.zeros((total,), jnp.float32), vector, base + place * vector.shape[0], 0)
        return whole.reshape(shards, total // shards)

    colsum = jnp.sum(dproj, axis=0)
    key_cols = colsum[wide : 2 * wide].reshape(wide // HD, HD)[:, :ROT].reshape(-1)
    pieces = [
        jnp.sum(dn_one * unit, axis=0).reshape(shards, share),
        jnp.sum(dn_one, axis=0).reshape(shards, share),
        jnp.sum(dn_two * unit, axis=0).reshape(shards, share),
        jnp.sum(dn_two, axis=0).reshape(shards, share),
        spread(colsum[:wide], 2 * D, 0) + spread(colsum[2 * wide :], 2 * D, D),
        spread(key_cols, H * ROT, 0),
        jnp.sum(cotangent.astype(jnp.float32), axis=(0, 1)).reshape(shards, share),
        spread(jnp.sum(dpre, axis=0), hidden * groups, 0),
    ]
    packed_grads = jnp.concatenate(pieces, axis=1)
    used = packed_grads.shape[1]
    more = -(-used // (4 * wide * 16)) * 16
    packed_grads = jnp.pad(packed_grads, ((0, 0), (0, more * 4 * wide - used)))
    attn_terms = jnp.concatenate([rows_dot(one_b, dproj_b), rows_dot(dy, mixed)], axis=1)
    attn_terms = jnp.concatenate(
        [attn_terms.reshape(shards, share, 4 * wide), packed_grads.reshape(shards, more, 4 * wide)],
        axis=1)
    attn_own = scatter_blocks(attn_terms.astype(jnp.bfloat16))
    ff_grads = lax.all_gather(ff_own, "ctx", axis=0)
    attn_grads = lax.all_gather(attn_own, "ctx", axis=0)

    qkv_grad = columns(attn_grads, share, 0, wide, 3)
    ao_grad = columns(attn_grads, share, 3 * wide, wide, 1)
    fi_grad = columns(ff_grads, share, 0, hidden, 1)
    fo_grad = columns(ff_grads, share, hidden, hidden, 1)
    vec = jnp.sum(attn_grads[:, share:].astype(jnp.float32), axis=0).reshape(-1)
    shares = []
    start = 0
    for piece in pieces:
        shares.append(vec[start : start + piece.shape[1]])
        start += piece.shape[1]
    return (
        layer_out,
        input_grad,
        shares[0],
        shares[1],
        shares[2],
        shares[3],
        qkv_grad,
        shares[4],
        shares[5],
        ao_grad,
        shares[6],
        fi_grad,
        shares[7],
        fo_grad,
        shares[6],
    )


def solution(mesh):
    placed = (
        P("fsdp", "ctx", None),
        P("fsdp", "ctx", None),
        P("fsdp"),
        P("fsdp"),
        P("fsdp"),
        P("fsdp"),
        P("fsdp", None),
        P("fsdp"),
        P("fsdp"),
        P("fsdp", None),
        P("fsdp"),
        P("fsdp", None),
        P("fsdp"),
        P("fsdp", None),
        P("fsdp"),
    )
    return jax.shard_map(
        per_device,
        mesh=mesh,
        in_specs=placed,
        out_specs=(
            P("fsdp", "ctx", None),
            P("fsdp", "ctx", None),
            P("fsdp"),
            P("fsdp"),
            P("fsdp"),
            P("fsdp"),
            P("fsdp", None),
            P("fsdp"),
            P("fsdp"),
            P("fsdp", None),
            P("fsdp"),
            P("fsdp", None),
            P("fsdp"),
            P("fsdp", None),
            P("fsdp"),
        ),
        check_vma=False,
    )
```
